256 devices in a mesh: grp: 32 (over y, x, core), mem: 8 (over z).
Axes of the slice: x: 4, y: 4, z: 8, core: 2. Of those that a mesh axis runs over, the one named last changes fastest.
Arguments:
- features: bfloat16 [131072, 512], P(('grp', 'mem')), may hold values from -6 to 6
- weight: bfloat16 [512, 512], replicated, may hold values from -0.25 to 0.25
- adj_tiles: bfloat16 [1024, 32, 128, 128], P(('grp', 'mem')), may hold values from -0.09375 to 0.09375
- adj_cols: int32 [1024, 32], P(('grp', 'mem')), may hold values from 0 to 31
- send_blocks: int32 [256, 32, 2], P(('grp', 'mem')), may hold values from -1 to 3, as said below
- read_tiles: bfloat16 [256, 32, 2, 128, 128], P(('grp', 'mem')), may hold values from -0.1875 to 0.1875
- read_rows: int32 [256, 32, 2], P(('grp', 'mem')), may hold values from 0 to 3
Outputs:
- output: bfloat16 [131072, 512], P(('grp', 'mem'))
The draws below stay inside these ranges and needn't reach their ends.
Inputs may be any that keep to these rules, and one draw needn't show every extreme that they name: `send_blocks`: -1 marks an empty slot; the used slots of each entry come first. In every draw, for each m some group receives 2 blocks from every vertex block s * 8 + m.
All inputs are finite; a program needn't handle non-finite values.
Results may differ from the reference program's by a relative error of at most 0.0058.
Values may be sent and summed in bfloat16 or wider, within the bound.
No kernel may reach another device: no remote copies, remote signals or barrier semaphores. Data moves between devices by JAX's collectives and lax.ppermute only.
A program may use at most 128 MiB of HBM per device.

```python
import jax
import jax.numpy as jnp
from jax import lax

F = 512
BLK = 128
KT = 32
CAP = 2
V_DEV = 512
NB = 4
V = 131072
N_GRP = 32
N_MEM = 8


def draw_send_blocks(key, part):
    device_count = N_GRP * N_MEM
    key_count = jax.random.fold_in(key, 11)
    key_hot = jax.random.fold_in(key, 23)
    key_block = jax.random.fold_in(key, 37)
    counts = jax.random.randint(key_count, (device_count, N_GRP), 0, CAP + 1)
    hot_group = jax.random.randint(key_hot, (N_MEM,), 0, N_GRP)
    device_index = jnp.arange(device_count, dtype=jnp.int32)
    hot_mask = jnp.arange(N_GRP, dtype=jnp.int32)[None, :] == hot_group[device_index % N_MEM][:, None]
    counts = jnp.where(hot_mask, CAP, counts)
    chosen = jax.random.randint(key_block, (device_count, N_GRP, CAP), 0, V_DEV // BLK)
    slot_index = jnp.arange(CAP, dtype=jnp.int32)
    return jnp.where(slot_index[None, None, :] < counts[:, :, None], chosen, -1).astype(jnp.int32)


def place_ends(entries, rng, low, largest):
    longest = entries.shape.index(max(entries.shape))
    spots = []
    for shift in (0, 1):
        where = [jax.random.randint(jax.random.fold_in(rng, axis), (), 0, length) for axis, length in enumerate(entries.shape)]
        where[longest] = (where[longest] + shift) % entries.shape[longest]
        spots.append(tuple(where))
    return entries.at[spots[0]].set(low).at[spots[1]].set(largest)


def block_levels(key, shape, split, least, largest):
    loudness, own = 1.0, jax.random.fold_in(key, 6)
    for dim, blocks in split:
        steps = jnp.exp(jax.random.uniform(jax.random.fold_in(own, dim), (blocks,), jnp.float32, least / len(split), largest / len(split)))
        loudness = loudness * jnp.repeat(steps, shape[dim] // blocks).reshape([-1 if axis == dim else 1 for axis in range(len(shape))])
    return loudness


def normal_values(stream_key, dims, scale, most, pieces=(), kind=jnp.bfloat16):
    result = scale * jax.random.normal(stream_key, dims, jnp.float32)
    if pieces:
        result = result * block_levels(stream_key, dims, pieces, -0.22, 0.18)
    return jnp.clip(result, -most, most).astype(kind)


def setup_inputs(seed: int = 0) -> dict:
    splits = jax.random.split(jax.random.key(seed), 8)
    features = normal_values(splits[0], (V, F), 1.0, 6.0, ((0, 256),))
    weight = normal_values(splits[1], (F, F), F ** -0.5, 0.25)
    adj_tiles = normal_values(splits[2], (V // BLK, KT, BLK, BLK), (KT * BLK) ** -0.5, 0.09375, ((0, 256),))
    adj_cols = place_ends(jax.random.randint(splits[3], (V // BLK, KT), 0, N_MEM * NB), jax.random.fold_in(splits[3], 1), 0, (N_MEM * NB) - 1).astype(jnp.int32)
    send_blocks = draw_send_blocks(jax.random.fold_in(splits[7], 71), 0)
    read_tiles = normal_values(splits[5], (N_GRP * N_MEM, N_GRP, CAP, BLK, BLK), (8 * BLK) ** -0.5, 0.1875, ((0, 256),))
    read_rows = place_ends(jax.random.randint(splits[6], (N_GRP * N_MEM, N_GRP, CAP), 0, NB), jax.random.fold_in(splits[6], 1), 0, NB - 1).astype(jnp.int32)
    return {"features": features, "weight": weight, "adj_tiles": adj_tiles, "adj_cols": adj_cols, "send_blocks": send_blocks, "read_tiles": read_tiles, "read_rows": read_rows}


def reference(features, weight, adj_tiles, adj_cols, send_blocks, read_tiles, read_rows):
    device_count = N_GRP * N_MEM
    block_count = V_DEV // BLK
    all_tiles = features.reshape(device_count * block_count, BLK, F)
    adj_all = adj_tiles.reshape(device_count, block_count, KT, BLK, BLK)
    cols_all = adj_cols.reshape(device_count, block_count, KT)

    def first_section(device):
        own_group = device // N_MEM
        base_tile = own_group * N_MEM * block_count
        chosen = all_tiles[base_tile + cols_all[device]]
        propagated = jnp.einsum('rkij,rkjf->rif', adj_all[device].astype(jnp.float32), chosen.astype(jnp.float32))
        propagated = propagated.astype(jnp.bfloat16).reshape(V_DEV, F)
        hidden = jnp.maximum(jnp.dot(propagated, weight, preferred_element_type=jnp.float32), 0.0)
        return hidden.astype(jnp.bfloat16)

    hidden_all = lax.map(first_section, jnp.arange(device_count, dtype=jnp.int32))
    hidden_tiles = hidden_all.reshape(device_count, block_count, BLK, F)

    def second_section(device):
        own_group = device // N_MEM
        member = device % N_MEM
        sources = jnp.arange(N_GRP, dtype=jnp.int32) * N_MEM + member
        slot_lists = send_blocks[sources, own_group]
        safe_lists = jnp.clip(slot_lists, 0, block_count - 1).astype(jnp.int32)
        received = hidden_tiles[sources[:, None], safe_lists]
        received = jnp.where((slot_lists >= 0)[:, :, None, None], received, jnp.zeros((), jnp.bfloat16))
        products = jnp.einsum('gkij,gkjf->gkif', read_tiles[device].astype(jnp.float32), received.astype(jnp.float32))
        onehot = (read_rows[device][:, :, None] == jnp.arange(block_count, dtype=jnp.int32)[None, None, :]).astype(jnp.float32)
        aggregate = jnp.einsum('gkr,gkif->rif', onehot, products, precision=lax.Precision.HIGHEST).reshape(V_DEV, F)
        return (hidden_all[device].astype(jnp.float32) + aggregate).astype(jnp.bfloat16)

    output = lax.map(second_section, jnp.arange(device_count, dtype=jnp.int32))
    return output.reshape(device_count * V_DEV, F)
```

```python
import jax
import jax.numpy as jnp
from jax import lax
from jax.experimental import pallas as pl
from jax.experimental.pallas import tpu as pltpu
from jax.sharding import PartitionSpec as P


NY, NX, NC, NM = 4, 4, 2, 8
BLK, F, V_DEV, NB = 128, 512, 512, 4
KT, CAP = 32, 2
MIB = 1 << 20
VMEM = pl.BlockSpec(memory_space=pltpu.VMEM)
SMEM = pl.BlockSpec(memory_space=pltpu.SMEM)

S_BASE = {0: 0, 1: 2, 3: 4, 2: 6}
LISTS = 10
SLOTS = 24
TRASH = 8


def grp_of(y, x, c):
    return ((y % NY) * NX + (x % NX)) * NC + c


GRID = [(y, x, c) for y in range(NY) for x in range(NX) for c in range(NC)]


def shift_x(v, d):
    return lax.ppermute(v, "grp", [(grp_of(y, x, c), grp_of(y, x + d, c)) for y, x, c in GRID])


def shift_y(v, d):
    return lax.ppermute(v, "grp", [(grp_of(y, x, c), grp_of(y + d, x, c)) for y, x, c in GRID])


def swap_core(v):
    return lax.ppermute(v, "grp", [(grp_of(y, x, c), grp_of(y, x, 1 - c)) for y, x, c in GRID])


def shift_z(v, d):
    return lax.ppermute(v, "mem", [(i, (i + d) % NM) for i in range(NM)])


def dense_body(cols, tiles, out, acc):
    r = pl.program_id(0)
    acc[...] = jnp.zeros_like(acc)

    def step(k, carry):
        c = cols[r * KT + k]
        acc[c] = acc[c] + tiles[0, k].astype(jnp.float32)
        return carry

    lax.fori_loop(0, KT, step, 0)
    for m in range(NM):
        for j in range(NB):
            out[m, :, j * BLK:(j + 1) * BLK] = acc[m * NB + j].astype(jnp.bfloat16)


def build_dense(cols, tiles):
    return pl.pallas_call(
        dense_body,
        grid_spec=pltpu.PrefetchScalarGridSpec(
            num_scalar_prefetch=1,
            grid=(NB,),
            in_specs=[pl.BlockSpec((1, KT, BLK, BLK), lambda r, c: (r, 0, 0, 0))],
            out_specs=pl.BlockSpec((NM, BLK, V_DEV), lambda r, c: (0, r, 0)),
            scratch_shapes=[pltpu.VMEM((KT, BLK, BLK), jnp.float32)],
        ),
        out_shape=jax.ShapeDtypeStruct((NM, V_DEV, V_DEV), jnp.bfloat16),
        compiler_params=pltpu.CompilerParams(vmem_limit_bytes=10 * MIB),
        cost_estimate=pl.CostEstimate(flops=4 * MIB, bytes_accessed=8 * MIB, transcendentals=0),
        name="dense_adjacency",
    )(cols, tiles)


def dot(a, b):
    return jnp.dot(a, b, preferred_element_type=jnp.float32)


def early_body(me, a, own, *refs):
    halves, out = refs[:-1], refs[-1]
    m = me[0]
    total = dot(a[m], own[...])
    for i, shift in enumerate((1, -1, 2, -2)):
        src = (m - shift + NM) % NM
        total += dot(a[src, :, :256], halves[2 * i][...])
        total += dot(a[src, :, 256:], halves[2 * i + 1][...])
    out[...] = total


def early_sum(me, a, own, halves):
    return pl.pallas_call(
        early_body,
        in_specs=[SMEM] + [VMEM] * (2 + len(halves)),
        out_specs=VMEM,
        out_shape=jax.ShapeDtypeStruct((V_DEV, F), jnp.float32),
        compiler_params=pltpu.CompilerParams(vmem_limit_bytes=12 * MIB),
        cost_estimate=pl.CostEstimate(flops=5 * 2 * 512**3, bytes_accessed=6 * MIB, transcendentals=0),
        name="early_sum",
    )(me, a, own, *halves)


def hidden_body(me, a, part, weight, *refs):
    halves, (out_a, out_b) = refs[:-2], refs[-2:]
    m = me[0]
    total = part[...]
    for i, shift in enumerate((3, -3, 4)):
        src = (m - shift + NM) % NM
        total += dot(a[src, :, :256], halves[2 * i][...])
        total += dot(a[src, :, 256:], halves[2 * i + 1][...])
    hidden = jnp.maximum(dot(total.astype(jnp.bfloat16), weight[...]), 0.0).astype(jnp.bfloat16)
    out_a[...] = hidden[:256]
    out_b[...] = hidden[256:]


def make_hidden(me, a, part, weight, halves):
    half = jax.ShapeDtypeStruct((V_DEV // 2, F), jnp.bfloat16)
    return pl.pallas_call(
        hidden_body,
        in_specs=[SMEM] + [VMEM] * (3 + len(halves)),
        out_specs=[VMEM, VMEM],
        out_shape=[half, half],
        compiler_params=pltpu.CompilerParams(vmem_limit_bytes=12 * MIB),
        cost_estimate=pl.CostEstimate(flops=4 * 2 * 512**3, bytes_accessed=8 * MIB, transcendentals=0),
        name="hidden",
    )(me, a, part, weight, *halves)


def list_of(first, second, colour):
    base = S_BASE[first]
    if second == 2:
        return 5 * colour + (3 if base < 4 else 4), base % 4
    return 5 * colour + {0: 0, 1: 1, 3: 2}[second], base


def plan_body(where, slots, rows, out):
    y, x, c = where[0], where[1], where[2]
    count = [jnp.int32(0)] * LISTS
    for dy in range(NY):
        for dx in range(NX):
            chip = ((y - dy + NY) % NY) * NX + (x - dx + NX) % NX
            for dest in range(NC):
                core = jnp.where(c == 0, dest, 1 - dest)
                for k in range(CAP):
                    j = slots[(dy * NX + dx) * 4 + core * CAP + k]
                    row = rows[dest * 32 + chip * CAP + k]
                    code = (dest * 32 + chip * CAP + k) * 16 + (dest * NB + row) * 1024
                    for colour in range(2):
                        which, base = list_of(dx, dy, 0) if colour == 0 else list_of(dy, dx, 1)
                        out[LISTS + which * SLOTS + count[which]] = code + base + j - 2 * colour
                        use = jnp.logical_and(j >= 2 * colour, j < 2 * colour + 2)
                        count[which] = count[which] + use.astype(jnp.int32)
    for which in range(LISTS):
        out[which] = count[which]
        for i in range(4):
            out[LISTS + which * SLOTS + count[which] + i] = jnp.int32(TRASH * 1024)


def make_plan(where, slots, rows):
    return pl.pallas_call(
        plan_body,
        in_specs=[SMEM] * 3,
        out_specs=SMEM,
        out_shape=jax.ShapeDtypeStruct((LISTS * (SLOTS + 1),), jnp.int32),
        cost_estimate=pl.CostEstimate(flops=MIB, bytes_accessed=MIB, transcendentals=0),
        name="plan",
    )(where, slots, rows)


def gather_sum(plan, tiles, acc, buffers, lists):
    for which, buf in zip(lists, buffers):
        def step(i, carry, which=which, buf=buf):
            for q in range(4):
                code = plan[LISTS + which * SLOTS + i * 4 + q]
                pos = pl.multiple_of((code & 15) * BLK, BLK)
                tile = (code >> 4) & 63
                slot = code >> 10
                acc[slot] = acc[slot] + dot(tiles[tile], buf[pl.ds(pos, BLK), :])
            return carry

        lax.fori_loop(0, (plan[which] + 3) // 4, step, 0)


def read_first_body(plan, tiles, *refs):
    buffers, acc = refs[:-1], refs[-1]
    acc[...] = jnp.zeros_like(acc)
    gather_sum(plan, tiles, acc, buffers, (0, 5))


def read_next_body(plan, tiles, given, *refs):
    buffers, acc = refs[:-1], refs[-1]
    acc[...] = given[...]
    gather_sum(plan, tiles, acc, buffers, (1, 2, 6, 7))


def read_last_body(plan, tiles, given, hid_a, hid_b, *refs):
    buffers, (mine, other), acc = refs[:-3], refs[-3:-1], refs[-1]
    acc[...] = given[...]
    gather_sum(plan, tiles, acc, buffers, (3, 4, 8, 9))
    for r in range(NB):
        half = (hid_a, hid_b)[r // 2]
        lo = (r % 2) * BLK
        mine[r * BLK:(r + 1) * BLK, :] = acc[r] + half[lo:lo + BLK, :].astype(jnp.float32)
        other[r * BLK:(r + 1) * BLK, :] = acc[NB + r].astype(jnp.bfloat16)


ACC = jax.ShapeDtypeStruct((2 * NB + 1, BLK, F), jnp.float32)


def read_call(body, args, n_flops, out_shape, out_specs, scratch=(), name=None):
    return pl.pallas_call(
        body,
        in_specs=[SMEM] + [VMEM] * (len(args) - 1),
        out_specs=out_specs,
        out_shape=out_shape,
        scratch_shapes=list(scratch),
        compiler_params=pltpu.CompilerParams(vmem_limit_bytes=20 * MIB),
        cost_estimate=pl.CostEstimate(flops=n_flops, bytes_accessed=4 * MIB, transcendentals=0),
        name=name,
    )(*args)


def first_phase(h, along):
    n = h.shape[0] // 2
    a, b = along(h, 1), along(h, -1)
    c1, c2 = along(a[:n], 1), along(b[n:], -1)
    return jnp.concatenate([h, a, b, c1, c2])


def per_device(features, weight, adj_tiles, adj_cols, send_blocks, read_tiles, read_rows):
    grp = lax.axis_index("grp").astype(jnp.int32)
    mem = lax.axis_index("mem").astype(jnp.int32)
    chip, core = grp // NC, grp % NC
    where = jnp.stack([chip // NX, chip % NX, core])
    me = mem[None]

    top, bottom = features[:256], features[256:]
    ups, downs = [(top, bottom)], [(top, bottom)]
    for _ in range(3):
        ups.append(tuple(shift_z(v, 1) for v in ups[-1]))
        downs.append(tuple(shift_z(v, -1) for v in downs[-1]))
    far = (shift_z(ups[3][0], 1), shift_z(downs[3][1], -1))

    tiles_in = read_tiles[0].reshape(NY * NX, NC, CAP, BLK, BLK)
    rows_in = read_rows[0].reshape(NY * NX, NC, CAP)
    own_tiles = lax.dynamic_index_in_dim(tiles_in, core, 1, keepdims=False)
    own_rows = lax.dynamic_index_in_dim(rows_in, core, 1, keepdims=False)
    other_tiles = swap_core(lax.dynamic_index_in_dim(tiles_in, 1 - core, 1, keepdims=False))
    other_rows = swap_core(lax.dynamic_index_in_dim(rows_in, 1 - core, 1, keepdims=False))
    tiles = jnp.concatenate([own_tiles, other_tiles]).reshape(-1, BLK, BLK)
    rows = jnp.concatenate([own_rows, other_rows]).reshape(-1)
    slots = send_blocks.reshape(1, -1)
    for shift, d in ((shift_x, 1), (shift_x, 2), (shift_y, 1), (shift_y, 2)):
        slots = jnp.concatenate([slots, shift(slots, d)])
    slots = lax.dynamic_slice_in_dim(slots, chip * NC * CAP, NC * CAP, 1).reshape(-1)
    plan = make_plan(where, slots, rows)

    dense = build_dense(adj_cols.reshape(-1), adj_tiles)
    part = early_sum(me, dense, features, [*ups[1], *downs[1], *ups[2], *downs[2]])
    hid_a, hid_b = make_hidden(me, dense, part, weight, [*ups[3], *downs[3], *far])

    bufs = []
    for h, one, two in ((hid_a, shift_x, shift_y), (hid_b, shift_y, shift_x)):
        s = first_phase(h, one)
        u, v = two(s, 1), two(s, -1)
        n = s.shape[0] // 2
        bufs.append((s, u, v, two(u[:n], 1), two(v[n:], -1)))
    (sa, ua, va, w1a, w2a), (sb, ub, vb, w1b, w2b) = bufs
    unit = 2 * BLK * BLK * F * 16
    acc = read_call(read_first_body, (plan, tiles, sa, sb), unit, ACC, VMEM, name="read_first")
    acc = read_call(read_next_body, (plan, tiles, acc, ua, va, ub, vb), 2 * unit, ACC, VMEM, name="read_next")
    mine, other = read_call(
        read_last_body, (plan, tiles, acc, hid_a, hid_b, w1a, w2a, w1b, w2b), unit,
        [jax.ShapeDtypeStruct((V_DEV, F), jnp.float32), jax.ShapeDtypeStruct((V_DEV, F), jnp.bfloat16)],
        [VMEM, VMEM], [pltpu.VMEM(ACC.shape, jnp.float32)], name="read_last")
    return (mine + swap_core(other).astype(jnp.float32)).astype(jnp.bfloat16)


def solution(mesh):
    placed = (
        P(("grp", "mem"), None),
        P(),
        P(("grp", "mem"), None, None, None),
        P(("grp", "mem"), None),
        P(("grp", "mem"), None, None),
        P(("grp", "mem"), None, None, None, None),
        P(("grp", "mem"), None, None),
    )
    return jax.shard_map(
        per_device, mesh=mesh, in_specs=placed, out_specs=P(("grp", "mem"), None), check_vma=False
    )
```

```python
import functools

import jax
import jax.numpy as jnp
from jax import lax
from jax.experimental import pallas as pl
from jax.experimental.pallas import tpu as pltpu
from jax.sharding import PartitionSpec as P


NY, NX, NC, NM = 4, 4, 2, 8
BLK, F, V_DEV, NB = 128, 512, 512, 4
KT, CAP = 32, 2
MIB = 1 << 20
VMEM = pl.BlockSpec(memory_space=pltpu.VMEM)
SMEM = pl.BlockSpec(memory_space=pltpu.SMEM)
HBM = pl.BlockSpec(memory_space=pltpu.HBM)

S_BASE = {0: (0, 0), 1: (0, 2), 3: (1, 0), 2: (1, 2)}
BUFFERS = 8
LISTS = 2 * BUFFERS
SLOTS = 12
TRASH = 8
UNROLL = 1


def grp_of(y, x, c):
    return ((y % NY) * NX + (x % NX)) * NC + c


GRID = [(y, x, c) for y in range(NY) for x in range(NX) for c in range(NC)]


def shift_x(v, d):
    return lax.ppermute(v, "grp", [(grp_of(y, x, c), grp_of(y, x + d, c)) for y, x, c in GRID])


def shift_y(v, d):
    return lax.ppermute(v, "grp", [(grp_of(y, x, c), grp_of(y + d, x, c)) for y, x, c in GRID])


def swap_core(v):
    return lax.ppermute(v, "grp", [(grp_of(y, x, c), grp_of(y, x, 1 - c)) for y, x, c in GRID])


def shift_z(v, d):
    return lax.ppermute(v, "mem", [(i, (i + d) % NM) for i in range(NM)])


def in_hbm(x):
    return pltpu.with_memory_space_constraint(x, pltpu.HBM)


def dense_body(r, cols, tiles, out, buf, acc, sem):
    copy = pltpu.make_async_copy(tiles.at[r], buf, sem)
    copy.start()
    acc[...] = jnp.zeros_like(acc)
    copy.wait()

    def step(k, carry):
        c = cols[r, k]
        acc[c] = acc[c] + buf[k].astype(jnp.float32)
        return carry

    lax.fori_loop(0, KT, step, 0)
    for m in range(NM):
        for j in range(NB):
            out[m, :, j * BLK:(j + 1) * BLK] = acc[m * NB + j].astype(jnp.bfloat16)


def build_dense(cols, tiles, r):
    return pl.pallas_call(
        functools.partial(dense_body, r),
        in_specs=[SMEM, HBM],
        out_specs=VMEM,
        scratch_shapes=[
            pltpu.VMEM((KT, BLK, BLK), jnp.bfloat16),
            pltpu.VMEM((KT, BLK, BLK), jnp.float32),
            pltpu.SemaphoreType.DMA,
        ],
        out_shape=jax.ShapeDtypeStruct((NM, BLK, V_DEV), jnp.bfloat16),
        compiler_params=pltpu.CompilerParams(vmem_limit_bytes=9 * MIB // 2),
        cost_estimate=pl.CostEstimate(flops=MIB, bytes_accessed=2 * MIB, transcendentals=0),
        name="dense_adjacency",
    )(cols, in_hbm(tiles))


def dot(a, b):
    return jnp.dot(a, b, preferred_element_type=jnp.float32)


def rows_of(dense, src):
    return jnp.concatenate([a[src] for a in dense])


def early_body(me, a0, a1, a2, a3, own, *refs):
    halves, out = refs[:-1], refs[-1]
    m = me[0]
    for i, dense in enumerate(((a0, a1), (a2, a3))):
        total = dot(rows_of(dense, m), own[...])
        for j, shift in enumerate((1, -1, 2, -2, 3, -3)):
            lhs = rows_of(dense, (m - shift + NM) % NM)
            total += dot(lhs[:, :256], halves[2 * j][...]) + dot(lhs[:, 256:], halves[2 * j + 1][...])
        out[i * 256:(i + 1) * 256, :] = total


def early_sum(me, dense, own, halves):
    return pl.pallas_call(
        early_body,
        in_specs=[SMEM] + [VMEM] * (5 + len(halves)),
        out_specs=VMEM,
        out_shape=jax.ShapeDtypeStruct((V_DEV, F), jnp.float32),
        compiler_params=pltpu.CompilerParams(vmem_limit_bytes=7 * MIB),
        cost_estimate=pl.CostEstimate(flops=7 * 2 * 512**3, bytes_accessed=6 * MIB, transcendentals=0),
        name="early_sum",
    )(me, *dense[:2], *map(in_hbm, dense[2:]), in_hbm(own), *halves)


def hidden_body(me, a0, a1, a2, a3, part, weight, first, second, *outs):
    src = (me[0] + NM // 2) % NM
    for i, (dense, out) in enumerate(zip(((a0, a1), (a2, a3)), outs)):
        lhs = rows_of(dense, src)
        total = part[i * 256:(i + 1) * 256, :]
        total += dot(lhs[:, :256], first[...]) + dot(lhs[:, 256:], second[...])
        out[...] = jnp.maximum(dot(total.astype(jnp.bfloat16), weight[...]), 0.0).astype(jnp.bfloat16)


def make_hidden(me, dense, part, weight, halves):
    half = jax.ShapeDtypeStruct((V_DEV // 2, F), jnp.bfloat16)
    return pl.pallas_call(
        hidden_body,
        in_specs=[SMEM] + [VMEM] * (6 + len(halves)),
        out_specs=[VMEM, VMEM],
        out_shape=[half, half],
        compiler_params=pltpu.CompilerParams(vmem_limit_bytes=7 * MIB),
        cost_estimate=pl.CostEstimate(flops=2 * 2 * 512**3, bytes_accessed=8 * MIB, transcendentals=0),
        name="hidden",
    )(me, *dense[:2], *map(in_hbm, dense[2:]), part, in_hbm(weight), *halves)


def list_of(first, second, colour):
    part, base = S_BASE[first]
    group = {0: 0, 1: 2, 3: 4, 2: 6}[second]
    return BUFFERS * colour + group + part, base


def plan_body(where, slots, own_rows, other_rows, out):
    y, x, c = where[0], where[1], where[2]
    count = [jnp.int32(0)] * LISTS
    for dy in range(NY):
        for dx in range(NX):
            chip = ((y - dy + NY) % NY) * NX + (x - dx + NX) % NX
            source = chip * NC + c
            places = [list_of(dx, dy, 0), list_of(dy, dx, 1)]

            def entry(e, counts, dy=dy, dx=dx, chip=chip, source=source, places=places):
                dest, k = e // CAP, e % CAP
                core = jnp.where(c == 0, dest, 1 - dest)
                j = slots[dy * NX + dx, core * CAP + k]
                row = jnp.where(dest == 0, own_rows[0, source * CAP + k], other_rows[0, source * CAP + k])
                code = (chip * CAP + k) * 4 + (dest * NB + row) * 128
                new = []
                for colour, (which, base) in enumerate(places):
                    out[LISTS + which * SLOTS + counts[colour]] = code + base + j - 2 * colour
                    use = jnp.logical_and(j >= 2 * colour, j < 2 * colour + 2)
                    new.append(counts[colour] + use.astype(jnp.int32))
                return tuple(new)

            done = lax.fori_loop(0, NC * CAP, entry, tuple(count[which] for which, _ in places))
            for (which, _), n in zip(places, done):
                count[which] = n
    for which in range(LISTS):
        out[which] = count[which]
        for i in range(UNROLL):
            out[LISTS + which * SLOTS + count[which] + i] = jnp.int32(TRASH * 128)


def make_plan(where, slots, own_rows, other_rows):
    return pl.pallas_call(
        plan_body,
        in_specs=[SMEM] * 4,
        out_specs=SMEM,
        out_shape=jax.ShapeDtypeStruct((LISTS * (SLOTS + 1),), jnp.int32),
        compiler_params=pltpu.CompilerParams(vmem_limit_bytes=MIB),
        cost_estimate=pl.CostEstimate(flops=MIB, bytes_accessed=MIB, transcendentals=0),
        name="plan",
    )(where, slots, own_rows, other_rows)


def gather_sum(plan, own, other, acc, buffers, lists):
    for which, buf in zip(lists, buffers):
        def step(i, carry, which=which, buf=buf):
            for q in range(UNROLL):
                code = plan[LISTS + which * SLOTS + i * UNROLL + q]
                pos = pl.multiple_of((code & 3) * BLK, BLK)
                tile = (code >> 2) & 31
                slot = code >> 7
                chip, k = tile // CAP, tile % CAP
                lhs = jnp.where(((slot >> 2) & 1) == 1, other[chip, k], own[chip, k])
                acc[slot] = acc[slot] + dot(lhs, buf[pl.ds(pos, BLK), :])
            return carry

        lax.fori_loop(0, (plan[which] + UNROLL - 1) // UNROLL, step, 0)


def lists_of(*parts):
    return [BUFFERS * colour + p for colour in range(2) for p in parts]


def read_first_body(plan, core, own_all, other_all, *refs):
    buffers, (acc, own, other, sems) = refs[:-4], refs[-4:]
    copies = [
        pltpu.make_async_copy(ref.at[:, core[0]], out, sems.at[i])
        for i, (ref, out) in enumerate(((own_all, own), (other_all, other)))]
    for copy in copies:
        copy.start()
    acc[...] = jnp.zeros_like(acc)
    for copy in copies:
        copy.wait()
    gather_sum(plan, own, other, acc, buffers, lists_of(0, 1))


def read_next_body(plan, own, other, given, *refs):
    buffers, acc = refs[:-1], refs[-1]
    acc[...] = given[...]
    gather_sum(plan, own, other, acc, buffers, lists_of(2, 3, 4, 5))


def read_last_body(plan, own, other, given, hid_a, hid_b, *refs):
    buffers, (mine, theirs), acc = refs[:-3], refs[-3:-1], refs[-1]
    acc[...] = given[...]
    gather_sum(plan, own, other, acc, buffers, lists_of(6, 7))
    for r in range(NB):
        half = (hid_a, hid_b)[r // 2]
        lo = (r % 2) * BLK
        mine[r * BLK:(r + 1) * BLK, :] = acc[r] + half[lo:lo + BLK, :].astype(jnp.float32)
        theirs[r * BLK:(r + 1) * BLK, :] = acc[NB + r].astype(jnp.bfloat16)


ACC = jax.ShapeDtypeStruct((2 * NB + 1, BLK, F), jnp.float32)


def read_call(body, args, n_flops, out_shape, out_specs, scratch=(), head=(SMEM,)):
    return pl.pallas_call(
        body,
        in_specs=[*head] + [VMEM] * (len(args) - len(head)),
        out_specs=out_specs,
        out_shape=out_shape,
        scratch_shapes=list(scratch),
        compiler_params=pltpu.CompilerParams(vmem_limit_bytes=20 * MIB),
        cost_estimate=pl.CostEstimate(flops=n_flops, bytes_accessed=4 * MIB, transcendentals=0),
    )(*args)


def pack_body(*refs):
    at = 0
    for ref in refs[:-1]:
        n = ref.shape[0]
        refs[-1][at:at + n, :] = ref[...]
        at += n


def pack(*parts):
    return pl.pallas_call(
        pack_body,
        in_specs=[VMEM] * len(parts),
        out_specs=VMEM,
        out_shape=jax.ShapeDtypeStruct((sum(p.shape[0] for p in parts), F), jnp.bfloat16),
        compiler_params=pltpu.CompilerParams(vmem_limit_bytes=3 * MIB),
        cost_estimate=pl.CostEstimate(flops=0, bytes_accessed=MIB // 2, transcendentals=0),
        name="pack",
    )(*parts)


def per_device(features, weight, adj_tiles, adj_cols, send_blocks, read_tiles, read_rows):
    grp = lax.axis_index("grp").astype(jnp.int32)
    mem = lax.axis_index("mem").astype(jnp.int32)
    chip, core = grp // NC, grp % NC
    where = jnp.stack([chip // NX, chip % NX, core])
    me = mem[None]

    slots = send_blocks.reshape(1, -1)

    up, down = [features[:256], features[256:]], [features[:256], features[256:]]
    ups, downs = [], []
    for _ in range(1, 4):
        up = [shift_z(v, 1) for v in up]
        down = [shift_z(v, -1) for v in down]
        ups.append(up)
        downs.append(down)
    far = (shift_z(up[0], 1), shift_z(down[1], -1))
    for shift, d in ((shift_x, 1), (shift_x, 2), (shift_y, 1), (shift_y, 2)):
        slots = jnp.concatenate([slots, shift(slots, d)])
    own_tiles = read_tiles.reshape(NY * NX, NC, CAP, BLK, BLK)
    other_tiles = swap_core(own_tiles)
    own_rows = read_rows.reshape(1, -1)
    other_rows = swap_core(own_rows)
    dense = [build_dense(adj_cols, adj_tiles, r) for r in range(NB)]
    part = early_sum(me, dense, features, [*ups[0], *downs[0], *ups[1], *downs[1], *ups[2], *downs[2]])
    slots = lax.dynamic_slice_in_dim(slots, chip * NC * CAP, NC * CAP, 1)
    plan = make_plan(where, slots, own_rows, other_rows)
    hid_a, hid_b = make_hidden(me, dense, part, weight, far)

    s1, s2, uv1, uv2, far1 = [], [], [], [], []
    for i, (h, one, two) in enumerate(((hid_a, shift_x, shift_y), (hid_b, shift_y, shift_x))):
        a, b = one(h, 1), one(h, -1)
        c, d = one(a[:BLK], 1), one(b[BLK:], -1)
        s1.append(pack(h, a))
        uv1.append((two(s1[i], 1), two(s1[i], -1)))
        s2.append(pack(b, c, d))
        uv2.append((two(s2[i], 1), two(s2[i], -1)))
        far1 += [two(uv1[i][0], 1), two(uv2[i][1], -1)]
    unit = 2 * BLK * BLK * F * 16
    half = jax.ShapeDtypeStruct((NY * NX, CAP, BLK, BLK), jnp.bfloat16)
    near = [b for st in zip(s1, s2) for b in st]
    acc, own, other = read_call(
        read_first_body, (plan, core[None], in_hbm(own_tiles), in_hbm(other_tiles), *near),
        unit, [ACC, half, half], [VMEM] * 3, [pltpu.SemaphoreType.DMA((2,))],
        head=(SMEM, SMEM, HBM, HBM))
    args = (plan, own, other)
    acc = read_call(read_next_body, (*args, acc, *[b for p, q in zip(uv1, uv2) for b in (p[0], q[0], p[1], q[1])]), 2 * unit, ACC, VMEM)
    mine, theirs = read_call(
        read_last_body, (*args, acc, hid_a, hid_b, *far1), unit,
        [jax.ShapeDtypeStruct((V_DEV, F), jnp.float32), jax.ShapeDtypeStruct((V_DEV, F), jnp.bfloat16)],
        [VMEM, VMEM], [pltpu.VMEM(ACC.shape, jnp.float32)])
    return (mine + swap_core(theirs).astype(jnp.float32)).astype(jnp.bfloat16)


def solution(mesh):
    placed = (
        P(("grp", "mem"), None),
        P(),
        P(("grp", "mem"), None, None, None),
        P(("grp", "mem"), None),
        P(("grp", "mem"), None, None),
        P(("grp", "mem"), None, None, None, None),
        P(("grp", "mem"), None, None),
    )
    return jax.shard_map(per_device, mesh=mesh, in_specs=placed, out_specs=P(("grp", "mem"), None), check_vma=False)
```
